32 devices in a mesh: shard: 8 (over z, x), rep: 4 (over y, core).
Axes of the slice: x: 2, y: 2, z: 4, core: 2. Of those that a mesh axis runs over, the one named last changes fastest.
Arguments:
- tokens_in: float32 [31520, 768], P(('shard', 'rep')), may hold values from -6 to 6
- routes: int32 [31520, 2], P(('shard', 'rep')), may hold values from 0 to 3, all different within a row; in each aligned block of 985 rows (0 to 984, 985 to 1969, ...) at most 616 rows name the same one
- first_gain: bfloat16 [768], P('shard'), may hold values from 0.5 to 1.5
- first_shift: bfloat16 [768], P('shard'), may hold values from -3 to 3
- joint_weight: bfloat16 [768, 2304], P('shard'), may hold values from -0.21875 to 0.21875
- joint_bias: bfloat16 [2, 768], P(None, 'shard'), may hold values from -3 to 3
- mixer_weight: bfloat16 [768, 768], P('shard'), may hold values from -0.625 to 0.625
- mixer_bias: bfloat16 [768], P('shard'), may hold values from -3 to 3
- second_gain: bfloat16 [768], P('shard'), may hold values from 0.5 to 1.5
- second_shift: bfloat16 [768], P('shard'), may hold values from -3 to 3
- router_weight: bfloat16 [768, 4], P('shard'), may hold values from -0.4375 to 0.4375
- expert_up: bfloat16 [4, 768, 3072], P(None, None, 'shard'), may hold values from -0.21875 to 0.21875
- upward_bias: bfloat16 [4, 3072], P(None, 'shard'), may hold values from -3 to 3
- expert_down: bfloat16 [4, 3072, 768], P(None, 'shard'), may hold values from -0.3125 to 0.3125
- downward_bias: bfloat16 [4, 768], P(None, 'shard'), may hold values from -3 to 3
- out_grad: float32 [31520, 768], P(('shard', 'rep')), may hold values from -6 to 6
Outputs:
- block_out: float32 [31520, 768], P(('shard', 'rep'))
- input_grad: float32 [31520, 768], P(('shard', 'rep'))
- first_gain_grad: float32 [768], P('shard')
- first_shift_grad: float32 [768], P('shard')
- joint_weight_grad: float32 [768, 2304], P('shard')
- joint_bias_grad: float32 [2, 768], P(None, 'shard')
- mixer_weight_grad: float32 [768, 768], P('shard')
- mixer_bias_grad: float32 [768], P('shard')
- second_gain_grad: float32 [768], P('shard')
- second_shift_grad: float32 [768], P('shard')
- router_weight_grad: float32 [768, 4], P('shard')
- expert_up_grad: float32 [4, 768, 3072], P(None, None, 'shard')
- upward_bias_grad: float32 [4, 3072], P(None, 'shard')
- expert_down_grad: float32 [4, 3072, 768], P(None, 'shard')
- downward_bias_grad: float32 [4, 768], P(None, 'shard')
The draws below stay inside these ranges and needn't reach their ends.
Inputs may be any that keep to these rules, and one draw needn't show every extreme that they name: `routes`: the two experts of a token differ. Among the rows of one device (985 aligned rows), no expert is named more than 616 times.
All inputs are finite; a program needn't handle non-finite values.
Results may differ from the reference program's by a relative error of at most 0.02.
Values may be sent and summed in bfloat16 or wider, within the bound.
A program may use at most 320 MiB of HBM per device.

```python
import math
import jax
import jax.numpy as jnp
import numpy as np
from jax import lax

D = 768
HEADS = 12
HEAD_DIM = 64
FF = 3072
SEQ = 197
EXPERTS = 4
TOK_DEV = 985
CAP = 616
TOKENS = 31520


def raised(values, rng, source, target, parts, factor):
    owner, partner = [(jnp.arange(values.shape[dim]) // (values.shape[dim] // parts)).reshape([-1 if axis == dim else 1 for axis in range(values.ndim)]) for dim in (source, target)]
    chosen = jax.random.permutation(rng, parts)[partner]
    strong = (owner == chosen) | (owner == (partner + parts // 2) % parts)
    return jnp.where(strong, factor * values, values)


def shard_levels(rng, extent, shards, low, top_value):
    factor_of, own = 1.0, jax.random.fold_in(rng, 6)
    for dim, shards_of in shards:
        draws = jnp.exp(jax.random.uniform(jax.random.fold_in(own, dim), (shards_of,), jnp.float32, low / len(shards), top_value / len(shards)))
        factor_of = factor_of * jnp.repeat(draws, extent[dim] // shards_of).reshape([-1 if axis == dim else 1 for axis in range(len(extent))])
    return factor_of


def routed_block(rng, own, number, rows, amount, top, bound, skew):
    order = jax.random.permutation(rng, amount)
    crowded, ordinary = load_shares(amount, rows * top, bound, skew, True), load_shares(amount, rows * top, bound, skew, False)
    places = jnp.arange(amount)

    def named(lengths, rotation):
        used = int((lengths > 0).sum())
        fixed = max(1, used // 4)
        moved = fixed + (places - fixed + rotation * (used - fixed)) % max(1, amount - fixed)
        return jnp.zeros((amount,), jnp.int32).at[order[jnp.where(places < fixed, places, moved)]].set(jnp.asarray(lengths, jnp.int32))

    lengths = jnp.where(number % 4 == 0, named(crowded, number // 4), named(ordinary, number - number // 4 - 1))
    mixed = jax.random.permutation(jax.random.fold_in(own, 3), amount)
    source_of, sink = mixed[0:amount // 2 * 2:2], mixed[1:amount // 2 * 2:2]
    slack = jnp.minimum(lengths[source_of] - 1, bound - lengths[sink]) // 2
    slack = jnp.where((source_of == order[0]) | (sink == order[0]) | (lengths[sink] == 0), 0, jnp.maximum(slack, 0))
    moved = jax.random.randint(jax.random.fold_in(own, 4), (amount // 2,), 0, 1 << 20) % (slack + 1)
    lengths = lengths.at[source_of].add(-moved).at[sink].add(moved)
    members = jnp.searchsorted(jnp.cumsum(lengths), jnp.arange(rows * top), side="right").astype(jnp.int32)
    table = members.reshape(top, rows).T
    table = table[jax.random.permutation(jax.random.fold_in(own, 1), rows)]
    rotation = jax.random.randint(jax.random.fold_in(own, 2), (rows, 1), 0, top)
    return jnp.take_along_axis(table, (jnp.arange(top)[None, :] + rotation) % top, axis=1)


def load_shares(number_of, total, bound, lean, full):
    loads = [(1 << 20) // math.isqrt(standing ** lean) + 1 for standing in range(1, number_of + 1)]
    largest = bound if full else min(bound, max(-(-total // number_of), total * loads[0] // sum(loads)))
    least = 1 if total - largest >= number_of - 1 else 0
    given, surplus = [largest] + [least] * (number_of - 1), total - largest - least * (number_of - 1)
    while surplus > 0:
        movable = [i for i in range(1, number_of) if given[i] < largest] or [i for i in range(1, number_of) if given[i] < bound]
        mass, remaining = sum([loads[i] for i in movable]), surplus
        for i in movable:
            addition = min(bound - given[i], max(1, remaining * loads[i] // mass), surplus)
            given[i] = given[i] + addition
            surplus = surplus - addition
    return np.array(given)


def bell_draw(own_key, dims, scale, bound, split=(), kind=jnp.bfloat16):
    factor_of = shard_levels(own_key, dims, split, -0.22, 0.18) if split else 1.0
    values = jax.random.normal(own_key, dims, jnp.float32) * scale * factor_of
    return jnp.minimum(jnp.maximum(values, -bound), bound).astype(kind)


def noise_with(key, shape, scale, limit, split, heavy, held_as=jnp.bfloat16):
    drawn = scale * jax.random.normal(key, shape, jnp.float32)
    if split:
        drawn = drawn * shard_levels(key, shape, split, -0.22, 0.18)
    return jnp.clip(raised(drawn, jax.random.fold_in(key, 3), *heavy), -limit, limit).astype(held_as)


def setup_inputs(seed: int = 0) -> dict:
    key_of = jax.random.split(jax.random.key(seed), 17)
    tokens_in = bell_draw(key_of[0], (TOKENS, D), 1.0, 6.0, ((0, 32),), jnp.float32)
    routes_keys = jax.random.split(jax.random.fold_in(key_of[1], 1), TOKENS // TOK_DEV)
    routes_turns = jax.random.permutation(jax.random.fold_in(key_of[1], 3), TOKENS // TOK_DEV)
    routes = jax.vmap(lambda own, number: routed_block(jax.random.fold_in(key_of[1], 2), own, number, TOK_DEV, EXPERTS, 2, CAP, 1))(routes_keys, routes_turns).reshape((TOKENS, 2))
    first_gain = jnp.clip(1.0 + 0.1 * jax.random.normal(key_of[2], (D,), jnp.float32), 0.5, 1.5).astype(jnp.bfloat16)
    first_shift = bell_draw(key_of[3], (D,), 0.5, 3.0, ((0, 8),))
    joint_weight = bell_draw(key_of[4], (D, 3 * D), D ** -0.5, 0.21875, ((0, 8),))
    joint_bias = bell_draw(key_of[5], (2, D), 0.5, 3.0, ((1, 8),))
    mixer_weight = bell_draw(key_of[6], (D, D), (D // 8) ** -0.5, 0.625, ((0, 8),))
    mixer_bias = bell_draw(key_of[7], (D,), 0.5, 3.0, ((0, 8),))
    second_gain = jnp.clip(1.0 + 0.1 * jax.random.normal(key_of[8], (D,), jnp.float32), 0.5, 1.5).astype(jnp.bfloat16)
    second_shift = bell_draw(key_of[9], (D,), 0.5, 3.0, ((0, 8),))
    router_weight = bell_draw(key_of[10], (D, EXPERTS), (D // 4) ** -0.5, 0.4375, ((0, 8),))
    expert_up = bell_draw(key_of[11], (EXPERTS, D, FF), D ** -0.5, 0.21875, ((2, 8),))
    upward_bias = bell_draw(key_of[12], (EXPERTS, FF), 0.5, 3.0, ((1, 8),))
    expert_down = bell_draw(key_of[13], (EXPERTS, FF, D), (FF // 8) ** -0.5, 0.3125, ((1, 8),))
    downward_bias = bell_draw(key_of[14], (EXPERTS, D), 0.5, 3.0, ((1, 8),))
    out_grad = noise_with(key_of[15], (TOKENS, D), 1.0, 6.0, ((0, 32),), (0, 1, 32, 2.75), jnp.float32)
    return dict(tokens_in=tokens_in, routes=routes, first_gain=first_gain, first_shift=first_shift, joint_weight=joint_weight, joint_bias=joint_bias, mixer_weight=mixer_weight, mixer_bias=mixer_bias, second_gain=second_gain, second_shift=second_shift, router_weight=router_weight, expert_up=expert_up, upward_bias=upward_bias, expert_down=expert_down, downward_bias=downward_bias, out_grad=out_grad)


@jax.custom_vjp
def low(v):
    return lax.optimization_barrier(v.astype(jnp.bfloat16)).astype(jnp.float32)

@jax.custom_vjp
def low_back(v):
    return v

def low_keep(v):
    return (low(v), None)

def low_pass(kept, grad):
    return (grad,)

def back_keep(v):
    return (v, None)

def back_low(kept, grad):
    return (low(grad),)
low.defvjp(low_keep, low_pass)
low_back.defvjp(back_keep, back_low)
epsilon = 1e-06
highest = lax.Precision.HIGHEST

def layer_norm(values, gain, shift):
    centre = lax.optimization_barrier(jnp.mean(values, axis=-1, keepdims=True))
    centred = values - centre
    spread = lax.optimization_barrier(jnp.mean(centred * centred, axis=-1, keepdims=True))
    return centred * lax.rsqrt(spread + epsilon) * gain + shift

def dispatch_tables(routes, experts, capacity):
    token_count = routes.shape[0]
    flat_routes = routes.reshape(-1).astype(jnp.int32)
    hit_table = (flat_routes[:, None] == jnp.arange(experts, dtype=jnp.int32)[None, :]).astype(jnp.int32)
    earlier = jnp.cumsum(hit_table, axis=0) - hit_table
    slot_index = lax.optimization_barrier(jnp.sum(earlier * hit_table, axis=1)).astype(jnp.int32)
    position = (flat_routes * capacity + slot_index).astype(jnp.int32)
    entries = jnp.arange(2 * token_count, dtype=jnp.int32)
    owner = jnp.full((experts * capacity,), 2 * token_count, jnp.int32).at[position].set(entries)
    return (position, owner)

def block_forward(weights, rows, route_rows):
    gain_one, shift_one, joint_full, joint_shift, mixer_full, mixer_shift, gain_two, shift_two, router_full, up_full, up_shift, down_full, down_shift = weights
    token_count, width = rows.shape
    images = token_count // SEQ
    head_scale = HEAD_DIM ** (-0.5)
    normed_one = low(layer_norm(rows, gain_one, shift_one))
    shift_all = jnp.concatenate([joint_shift[0], jnp.zeros((width,), jnp.float32), joint_shift[1]])
    projected = low(low_back(jnp.dot(normed_one, joint_full, precision=highest) + shift_all))
    parted = projected.reshape(images, SEQ, 3, HEADS, HEAD_DIM)
    queries = parted[:, :, 0]
    key_rows = parted[:, :, 1]
    value_rows = parted[:, :, 2]
    scores = low_back(jnp.einsum('bqhd,bkhd->bhqk', queries, key_rows, precision=highest) * head_scale)
    attention = low(jax.nn.softmax(scores, axis=-1))
    mixed = jnp.einsum('bhqk,bkhd->bqhd', attention, value_rows, precision=highest).reshape(token_count, width)
    mixed = low(low_back(mixed))
    branch_one = low_back(jnp.dot(mixed, mixer_full, precision=highest) + mixer_shift)
    residual_one = rows + branch_one
    normed_two = low(layer_norm(residual_one, gain_two, shift_two))
    logits = low_back(jnp.dot(normed_two, router_full, precision=highest))
    router_probs = jax.nn.softmax(logits, axis=-1)
    experts = up_full.shape[0]
    position, owner = dispatch_tables(route_rows, experts, CAP)
    choose = (route_rows[:, :, None] == jnp.arange(experts, dtype=jnp.int32)[None, None, :]).astype(jnp.float32)
    gates = lax.optimization_barrier(jnp.sum(choose * router_probs[:, None, :], axis=-1))
    padded = jnp.concatenate([normed_two, jnp.zeros((1, width), jnp.float32)], axis=0)
    dispatched = padded[owner // 2].reshape(experts, CAP, width)
    hidden = low_back(jnp.einsum('ecd,edf->ecf', dispatched, up_full, precision=highest) + up_shift[:, None, :])
    active = low(jax.nn.gelu(hidden, approximate=False))
    expert_result = low_back(jnp.einsum('ecf,efd->ecd', active, down_full, precision=highest) + down_shift[:, None, :])
    picked = expert_result.reshape(experts * CAP, width)[position].reshape(token_count, 2, width)
    return residual_one + lax.optimization_barrier(jnp.sum(gates[:, :, None] * picked, axis=1))

def reference(tokens_in, routes, first_gain, first_shift, joint_weight, joint_bias, mixer_weight, mixer_bias, second_gain, second_shift, router_weight, expert_up, upward_bias, expert_down, downward_bias, out_grad):
    raw_params = (first_gain, first_shift, joint_weight, joint_bias, mixer_weight, mixer_bias, second_gain, second_shift, router_weight, expert_up, upward_bias, expert_down, downward_bias)
    params = tuple((weight_array.astype(jnp.float32) for weight_array in raw_params))
    block_count = TOKENS // TOK_DEV
    token_blocks = tokens_in.reshape(block_count, TOK_DEV, D)
    route_blocks = routes.reshape(block_count, TOK_DEV, 2)
    grad_blocks = out_grad.reshape(block_count, TOK_DEV, D)
    checked = jax.checkpoint(block_forward)

    def visit(totals, inputs):
        block_tokens, block_routes, block_grad = inputs

        def forward(weights, rows):
            return checked(weights, rows, block_routes)
        result, pullback = jax.vjp(forward, params, block_tokens)
        weight_grads, token_grads = pullback(block_grad)
        totals = jax.tree.map(lambda earlier_sum, block_sum: earlier_sum + block_sum, totals, weight_grads)
        return (totals, (result, token_grads))
    start_totals = jax.tree.map(jnp.zeros_like, params)
    totals, (outputs, token_grads) = lax.scan(visit, start_totals, (token_blocks, route_blocks, grad_blocks))
    block_out = outputs.reshape(TOKENS, D)
    input_grad = token_grads.reshape(TOKENS, D)
    return (block_out, input_grad, totals[0], totals[1], totals[2], totals[3], totals[4], totals[5], totals[6], totals[7], totals[8], totals[9], totals[10], totals[11], totals[12])
```

```python
import functools

import jax
import jax.numpy as jnp
from jax import lax
from jax.sharding import PartitionSpec as P

HEADS = 12
HEAD_DIM = 64
SEQ = 197
CAP = 616


epsilon = 1e-06


def layer_norm(values, gain, shift):
    centre = jnp.mean(values, axis=-1, keepdims=True)
    centred = values - centre
    spread = jnp.mean(centred * centred, axis=-1, keepdims=True)
    factor = lax.rsqrt(spread + epsilon)
    unit_rows = centred * factor
    return (unit_rows * gain + shift, unit_rows, factor)


def norm_back(upstream, unit_rows, factor, gain):
    scaled = upstream * gain
    middle = jnp.mean(scaled, axis=-1, keepdims=True)
    along = jnp.mean(scaled * unit_rows, axis=-1, keepdims=True)
    return factor * (scaled - middle - unit_rows * along)


def contract_first(left_rows, right_rows):
    return lax.dot_general(
        left_rows, right_rows, (((0,), (0,)), ((), ())), preferred_element_type=jnp.float32
    )


def contract_last(left_rows, right_rows):
    return lax.dot_general(
        left_rows, right_rows, (((1,), (1,)), ((), ())), preferred_element_type=jnp.float32
    )


def slot_table(routes, experts, capacity):
    token_count = routes.shape[0]
    hits = (routes[:, :, None] == jnp.arange(experts, dtype=jnp.int32)[None, None, :]).any(axis=1)
    rows = lax.broadcasted_iota(jnp.int32, (token_count, token_count), 0)
    columns = lax.broadcasted_iota(jnp.int32, (token_count, token_count), 1)
    earlier = jnp.dot(
        (columns < rows).astype(jnp.bfloat16),
        hits.astype(jnp.bfloat16),
        preferred_element_type=jnp.float32,
    ).astype(jnp.int32)
    slot_of = jnp.where(hits, earlier, -1).T
    return slot_of[:, None, :] == jnp.arange(capacity, dtype=jnp.int32)[None, :, None]


def gather_all(piece):
    return lax.all_gather(piece, ("shard", "rep"), axis=0, tiled=True)


def my_piece(rows, copies):
    count = rows.shape[0] // copies
    return lax.dynamic_slice_in_dim(rows, lax.axis_index("rep") * count, count, axis=0)


def sum_rows(rows):
    return lax.psum_scatter(rows, ("shard", "rep"), scatter_dimension=0, tiled=True)


def share_rows(rows):
    return lax.all_gather(rows, "rep", axis=0, tiled=True)


def shards(
    tokens_in,
    routes,
    first_gain,
    first_shift,
    joint_weight,
    joint_bias,
    mixer_weight,
    mixer_bias,
    second_gain,
    second_shift,
    router_weight,
    expert_up,
    upward_bias,
    expert_down,
    downward_bias,
    out_grad,
    *,
    groups,
    copies,
):
    token_count, width = tokens_in.shape
    experts, _, part = expert_up.shape
    strip = first_gain.shape[0]
    hidden_width = part * groups
    images = token_count // SEQ
    capacity = CAP
    head_scale = HEAD_DIM ** (-0.5)
    low = jnp.bfloat16
    bias_columns = experts * part // strip

    packed = jnp.concatenate(
        [
            joint_weight,
            mixer_weight,
            router_weight,
            first_gain[:, None],
            first_shift[:, None],
            joint_bias.T,
            mixer_bias[:, None],
            second_gain[:, None],
            second_shift[:, None],
            downward_bias.T,
            upward_bias.reshape(strip, bias_columns),
        ],
        axis=1,
    )
    used = packed.shape[1]
    packed_width = -(-used // 128) * 128
    packed = jnp.pad(packed, ((0, 0), (0, packed_width - used)))
    packed = gather_all(my_piece(packed, copies))
    up_full = gather_all(my_piece(expert_up.reshape(experts * width, part), copies))
    up_full = up_full.reshape(groups, experts, width, part).transpose(1, 2, 0, 3)
    up_full = up_full.reshape(experts, width, hidden_width)
    down_full = gather_all(my_piece(expert_down.reshape(experts * part, width), copies))
    down_full = down_full.reshape(groups, experts, part, width).transpose(1, 0, 2, 3)
    down_full = down_full.reshape(experts, hidden_width, width)

    joint_full = packed[:, : 3 * width]
    mixer_full = packed[:, 3 * width : 4 * width]
    tail = packed[:, 4 * width :]
    router_full = tail[:, :experts]
    vectors = tail[:, experts : experts + 7].astype(jnp.float32).T
    gain_one, shift_one, shift_query, shift_value, mixer_shift, gain_two, shift_two = [
        vectors[i] for i in range(7)
    ]
    down_shift = tail[:, experts + 7 : 2 * experts + 7].astype(jnp.float32).T
    up_shift = (
        tail[:, 2 * experts + 7 : 2 * experts + 7 + bias_columns]
        .reshape(groups, experts, part)
        .transpose(1, 0, 2)
        .reshape(experts, hidden_width)
        .astype(jnp.float32)
    )
    normed_one, unit_one, factor_one = layer_norm(tokens_in, gain_one, shift_one)
    normed_one = normed_one.astype(low)
    shift_all = jnp.concatenate([shift_query, jnp.zeros((width,), jnp.float32), shift_value])
    projected = (
        jnp.dot(normed_one, joint_full, preferred_element_type=jnp.float32) + shift_all
    ).astype(low)
    parted = projected.reshape(images, SEQ, 3, HEADS, HEAD_DIM)
    queries = parted[:, :, 0]
    key_rows = parted[:, :, 1]
    value_rows = parted[:, :, 2]
    scores = (
        jnp.einsum("bqhd,bkhd->bhqk", queries, key_rows, preferred_element_type=jnp.float32)
        * head_scale
    )
    highest_score = jnp.max(scores, axis=-1, keepdims=True)
    log_total = highest_score + jnp.log(
        jnp.sum(jnp.exp(scores - highest_score), axis=-1, keepdims=True)
    )
    attention = jnp.exp(scores - log_total).astype(low)
    mixed = jnp.einsum("bhqk,bkhd->bqhd", attention, value_rows, preferred_element_type=jnp.float32)
    mixed = mixed.reshape(token_count, width).astype(low)
    residual_one = tokens_in + (
        jnp.dot(mixed, mixer_full, preferred_element_type=jnp.float32) + mixer_shift
    )
    normed_two, unit_two, factor_two = layer_norm(residual_one, gain_two, shift_two)
    normed_two = normed_two.astype(low)
    logits = jnp.dot(normed_two, router_full, preferred_element_type=jnp.float32)
    router_probs = jax.nn.softmax(logits, axis=-1)

    seated = slot_table(routes, experts, capacity)
    seats = seated.astype(low)
    flat_seats = seats.reshape(experts * capacity, token_count)
    gate_slots = jnp.sum(jnp.where(seated, router_probs.T[:, None, :], 0.0), axis=-1)[:, :, None]
    dispatched = (
        jnp.dot(flat_seats, normed_two, preferred_element_type=jnp.float32)
        .astype(low)
        .reshape(experts, capacity, width)
    )
    grad_slots = jnp.dot(
        flat_seats, out_grad.astype(low), preferred_element_type=jnp.float32
    ).reshape(experts, capacity, width)
    result_grad = (gate_slots * grad_slots).astype(low)

    hidden = (
        jnp.einsum("ecd,edf->ecf", dispatched, up_full, preferred_element_type=jnp.float32)
        + up_shift[:, None, :]
    )
    normal_cdf = 0.5 * (1.0 + lax.erf(hidden * 0.7071067811865476))
    active = (hidden * normal_cdf).astype(low)
    density = jnp.exp(-0.5 * hidden * hidden) * 0.3989422804014327
    active_grad = jnp.einsum(
        "ecd,efd->ecf", result_grad, down_full, preferred_element_type=jnp.float32
    )
    hidden_grad = (active_grad * (normal_cdf + hidden * density)).astype(low)
    up_grad = jnp.einsum(
        "ecd,ecf->edf", dispatched, hidden_grad, preferred_element_type=jnp.float32
    ).astype(low)
    up_grad = up_grad.reshape(experts, width, groups, part).transpose(2, 0, 1, 3)
    up_grad = sum_rows(up_grad.reshape(groups * experts * width, part))
    down_grad = jnp.einsum(
        "ecf,ecd->efd", active, result_grad, preferred_element_type=jnp.float32
    ).astype(low)
    down_grad = down_grad.reshape(experts, groups, part, width).transpose(1, 0, 2, 3)
    down_grad = sum_rows(down_grad.reshape(groups * experts * part, width))
    up_grad = share_rows(up_grad).astype(jnp.float32).reshape(experts, width, part)
    down_grad = share_rows(down_grad).astype(jnp.float32).reshape(experts, part, width)

    expert_result = (
        jnp.einsum("ecf,efd->ecd", active, down_full, preferred_element_type=jnp.float32)
        + down_shift[:, None, :]
    )
    gate_grad = jnp.sum(grad_slots * expert_result, axis=-1)
    weighted = (gate_slots * expert_result).astype(low).reshape(experts * capacity, width)
    block_out = residual_one + contract_first(flat_seats, weighted)
    probs_grad = jnp.sum(jnp.where(seated, gate_grad[:, :, None], 0.0), axis=1).T
    logit_grad = (
        router_probs * (probs_grad - jnp.sum(router_probs * probs_grad, axis=-1, keepdims=True))
    ).astype(low)
    router_grad = contract_first(normed_two, logit_grad)
    down_shift_grad = jnp.sum(result_grad.astype(jnp.float32), axis=1)
    up_shift_grad = jnp.sum(hidden_grad.astype(jnp.float32), axis=1)
    dispatched_grad = jnp.einsum(
        "ecf,edf->ecd", hidden_grad, up_full, preferred_element_type=jnp.float32
    )
    normed_grad = contract_last(logit_grad, router_full) + contract_first(
        flat_seats, dispatched_grad.astype(low).reshape(experts * capacity, width)
    )
    gain_two_grad = jnp.sum(normed_grad * unit_two, axis=0)
    shift_two_grad = jnp.sum(normed_grad, axis=0)
    residual_grad = out_grad + norm_back(normed_grad, unit_two, factor_two, gain_two)
    mixer_in_grad = residual_grad.astype(low)
    mixer_shift_grad = jnp.sum(mixer_in_grad.astype(jnp.float32), axis=0)
    mixer_grad = contract_first(mixed, mixer_in_grad)
    mixed_grad = (
        contract_last(mixer_in_grad, mixer_full)
        .astype(low)
        .reshape(images, SEQ, HEADS, HEAD_DIM)
    )
    scores_again = (
        jnp.einsum("bqhd,bkhd->bhqk", queries, key_rows, preferred_element_type=jnp.float32)
        * head_scale
    )
    attention_full = jnp.exp(scores_again - log_total)
    attention_low = attention_full.astype(low)
    weight_grad = jnp.einsum(
        "bqhd,bkhd->bhqk", mixed_grad, value_rows, preferred_element_type=jnp.float32
    )
    centre_grad = jnp.sum(attention_full * weight_grad, axis=-1, keepdims=True)
    score_grad = (attention_full * (weight_grad - centre_grad)).astype(low)
    query_grad = (
        jnp.einsum("bhqk,bkhd->bqhd", score_grad, key_rows, preferred_element_type=jnp.float32)
        * head_scale
    ).astype(low)
    key_grad = (
        jnp.einsum("bhqk,bqhd->bkhd", score_grad, queries, preferred_element_type=jnp.float32)
        * head_scale
    ).astype(low)
    value_grad = jnp.einsum(
        "bhqk,bqhd->bkhd", attention_low, mixed_grad, preferred_element_type=jnp.float32
    ).astype(low)
    projected_grad = jnp.concatenate(
        [
            query_grad.reshape(token_count, width),
            key_grad.reshape(token_count, width),
            value_grad.reshape(token_count, width),
        ],
        axis=1,
    )
    joint_sums = jnp.sum(projected_grad.astype(jnp.float32), axis=0)
    joint_grad = contract_first(normed_one, projected_grad)
    first_grad = contract_last(projected_grad, joint_full)
    gain_one_grad = jnp.sum(first_grad * unit_one, axis=0)
    shift_one_grad = jnp.sum(first_grad, axis=0)
    input_grad = residual_grad + norm_back(first_grad, unit_one, factor_one, gain_one)

    small = jnp.stack(
        [
            gain_one_grad,
            shift_one_grad,
            joint_sums[:width],
            joint_sums[2 * width :],
            mixer_shift_grad,
            gain_two_grad,
            shift_two_grad,
        ],
        axis=1,
    )
    packed_grad = jnp.concatenate(
        [
            joint_grad.astype(low),
            mixer_grad.astype(low),
            router_grad.astype(low),
            small.astype(low),
            down_shift_grad.T.astype(low),
            up_shift_grad.astype(low)
            .reshape(experts, groups, part)
            .transpose(1, 0, 2)
            .reshape(groups * strip, bias_columns),
        ],
        axis=1,
    )
    packed_grad = jnp.pad(packed_grad, ((0, 0), (0, packed_width - used)))
    packed_grad = share_rows(sum_rows(packed_grad)).astype(jnp.float32)
    end = packed_grad[:, 4 * width :]
    line = end[:, experts : experts + 7].T
    return (
        block_out,
        input_grad,
        line[0],
        line[1],
        packed_grad[:, : 3 * width],
        line[2:4],
        packed_grad[:, 3 * width : 4 * width],
        line[4],
        line[5],
        line[6],
        end[:, :experts],
        up_grad,
        end[:, 2 * experts + 7 : 2 * experts + 7 + bias_columns].reshape(experts, part),
        down_grad,
        end[:, experts + 7 : 2 * experts + 7].T,
    )


def solution(mesh):
    placed = (
        P(("shard", "rep"), None),
        P(("shard", "rep"), None),
        P("shard"),
        P("shard"),
        P("shard", None),
        P(None, "shard"),
        P("shard", None),
        P("shard"),
        P("shard"),
        P("shard"),
        P("shard", None),
        P(None, None, "shard"),
        P(None, "shard"),
        P(None, "shard", None),
        P(None, "shard"),
        P(("shard", "rep"), None),
    )
    return jax.shard_map(
        functools.partial(
            shards, groups=mesh.shape["shard"], copies=mesh.shape["rep"]
        ),
        mesh=mesh,
        in_specs=placed,
        out_specs=(
            P(("shard", "rep"), None),
            P(("shard", "rep"), None),
            P("shard"),
            P("shard"),
            P("shard", None),
            P(None, "shard"),
            P("shard", None),
            P("shard"),
            P("shard"),
            P("shard"),
            P("shard", None),
            P(None, None, "shard"),
            P(None, "shard"),
            P(None, "shard", None),
            P(None, "shard"),
        ),
        check_vma=False,
    )
```
